32 devices in a mesh: dp: 8 (over z, x), tensor: 4 (over y, core).
Axes of the slice: x: 2, y: 2, z: 4, core: 2. Of those that a mesh axis runs over, the one named last changes fastest.
Arguments:
- block_in: bfloat16 [20480, 1536], P(('dp', 'tensor')), may hold values from -10 to 10
- cotangent: bfloat16 [20480, 1536], P(('dp', 'tensor')), may hold values from -6 to 6
- seq_lengths: int32 [8, 2], P('dp'), may hold values from 1024 to 1280, as said below
- seq_offsets: int32 [8, 2], P('dp'), may hold values from 0 to 1280, as said below
- tok_counts: int32 [8, 4], P('dp', 'tensor'), may hold values from 128 to 640, as said below
- norm1_gain: bfloat16 [1536], P('dp'), may hold values from 0.5 to 1.5
- norm2_gain: bfloat16 [1536], P('dp'), may hold values from 0.5 to 1.5
- w_query: bfloat16 [1536, 1536], P('dp', 'tensor'), may hold values from -5 to 5
- w_key: bfloat16 [1536, 768], P('dp', 'tensor'), may hold values from -5 to 5
- w_value: bfloat16 [1536, 768], P('dp', 'tensor'), may hold values from -0.15625 to 0.15625
- w_out: bfloat16 [1536, 1536], P('tensor', 'dp'), may hold values from -1.25 to 1.25
- w_gate: bfloat16 [1536, 4096], P('dp', 'tensor'), may hold values from -0.15625 to 0.15625
- w_up: bfloat16 [1536, 4096], P('dp', 'tensor'), may hold values from -0.15625 to 0.15625
- w_down: bfloat16 [4096, 1536], P('tensor', 'dp'), may hold values from -0.09375 to 0.09375
Outputs:
- block_out: bfloat16 [20480, 1536], P(('dp', 'tensor'))
- grad_input: float32 [20480, 1536], P(('dp', 'tensor'))
- grad_norm1_gain: float32 [1536], P('dp')
- grad_norm2_gain: float32 [1536], P('dp')
- grad_w_query: float32 [1536, 1536], P('dp', 'tensor')
- grad_w_key: float32 [1536, 768], P('dp', 'tensor')
- grad_w_value: float32 [1536, 768], P('dp', 'tensor')
- grad_w_out: float32 [1536, 1536], P('tensor', 'dp')
- grad_w_gate: float32 [1536, 4096], P('dp', 'tensor')
- grad_w_up: float32 [1536, 4096], P('dp', 'tensor')
- grad_w_down: float32 [4096, 1536], P('tensor', 'dp')
The draws below stay inside these ranges and needn't reach their ends.
Inputs may be any that keep to these rules, and one draw needn't show every extreme that they name: `seq_lengths`: every draw has a sequence of exactly 1280 tokens and a group whose sequences all have exactly 1024. A group's sequences follow one another from its first row: seq_offsets[g, 0] = 0 and seq_offsets[g, s + 1] = seq_offsets[g, s] + seq_lengths[g, s]. tok_counts[g, t] is group g's total length minus t * 640, limited to 0 to 640.
All inputs are finite; a program needn't handle non-finite values.
Results may differ from the reference program's by a relative error of at most 0.014.
The reference program's roundings to bfloat16 on the way count: a program that leaves them out, or rounds other values in their place, can miss the bound.
Values may be sent and summed in bfloat16 or wider, within the bound.
A program may use at most 256 MiB of HBM per device.

```python
import jax
import jax.numpy as jnp
from jax import lax

D = 1536
HEADS = 16
KV_HEADS = 8
HD = 96
FF = 4096
SEQ_GRP = 2
MAXLEN = 1280
MINLEN = 1024
CAP = 2560
ROWS = 640
GROUPS = 8
TOKENS = 20480


def packing(key):
    base = jax.random.fold_in(key, 5021)
    lengths = jax.random.randint(jax.random.fold_in(base, 1), (GROUPS, SEQ_GRP), MINLEN, MAXLEN + 1, dtype=jnp.int32)
    chosen = jax.random.randint(jax.random.fold_in(base, 2), (), 0, GROUPS, dtype=jnp.int32)
    second = (chosen + 1) % GROUPS
    lengths = lengths.at[second, :].set(MINLEN)
    lengths = lengths.at[chosen, 0].set(MAXLEN)
    lengths = lengths.at[chosen, SEQ_GRP - 1].set(MINLEN)
    offsets = jnp.cumsum(lengths, axis=1) - lengths
    totals = jnp.sum(lengths, axis=1)
    firsts = jnp.arange(CAP // ROWS, dtype=jnp.int32) * ROWS
    counts = jnp.clip(totals[:, None] - firsts[None, :], 0, ROWS)
    return (lengths.astype(jnp.int32), offsets.astype(jnp.int32), counts.astype(jnp.int32))


def draw_seq_lengths(key, part):
    return packing(key)[0]


def draw_seq_offsets(key, part):
    return packing(key)[1]


def draw_tok_counts(key, part):
    return packing(key)[2]


def draw_block_in(key, part):
    values = jnp.clip(jax.random.normal(jax.random.fold_in(key, 13), (TOKENS, D), jnp.float32), -6.0, 6.0)
    return values.astype(jnp.bfloat16)


def draw_w_query(key, part):
    noise = jnp.clip(jax.random.normal(jax.random.fold_in(key, 11), (D, HEADS * HD), jnp.float32), -4.0, 4.0) * D ** (-0.5)
    return noise.astype(jnp.bfloat16)


def draw_w_key(key, part):
    noise = jnp.clip(jax.random.normal(jax.random.fold_in(key, 12), (D, KV_HEADS * HD), jnp.float32), -4.0, 4.0) * D ** (-0.5)
    return noise.astype(jnp.bfloat16)


def spiked(drawn, stream_key, source, target, blocks, factor):
    owner, partner = [(jnp.arange(drawn.shape[axis_at]) // (drawn.shape[axis_at] // blocks)).reshape([-1 if axis == axis_at else 1 for axis in range(drawn.ndim)]) for axis_at in (source, target)]
    chosen = jax.random.permutation(stream_key, blocks)[partner]
    strong = (owner == chosen) | (owner == (partner + blocks // 2) % blocks)
    return jnp.where(strong, factor * drawn, drawn)


def block_scale(key, dims, cuts, smallest, top_value):
    loudness, own = 1.0, jax.random.fold_in(key, 6)
    for dim, parts in cuts:
        draws = jnp.exp(jax.random.uniform(jax.random.fold_in(own, dim), (parts,), jnp.float32, smallest / len(cuts), top_value / len(cuts)))
        loudness = loudness * jnp.repeat(draws, dims[dim] // parts).reshape([-1 if axis == dim else 1 for axis in range(len(dims))])
    return loudness


def bell_draw(own_key, shape, deviation, reach, shards=(), kind=jnp.bfloat16):
    entries = jax.random.normal(own_key, shape, jnp.float32) * deviation
    if len(shards) > 0:
        entries = block_scale(own_key, shape, shards, -0.22, 0.18) * entries
    return jnp.clip(entries, min=-reach, max=reach).astype(kind)


def heavy_noise(rng, extent, width, limit, pieces, heavy, kind=jnp.bfloat16):
    drawn = width * jax.random.normal(rng, extent, jnp.float32)
    if pieces:
        drawn = drawn * block_scale(rng, extent, pieces, -0.22, 0.18)
    return jnp.clip(spiked(drawn, jax.random.fold_in(rng, 3), *heavy), -limit, limit).astype(kind)


def setup_inputs(seed: int = 0) -> dict:
    splits = jax.random.split(jax.random.key(seed), 15)
    return {
        "block_in": draw_block_in(jax.random.fold_in(splits[14], 71), 0),
        "cotangent": heavy_noise(splits[1], (TOKENS, D), 1.0, 6.0, ((0, 32),), (0, 1, 32, 2.75)),
        "seq_lengths": draw_seq_lengths(jax.random.fold_in(splits[14], 71), 0),
        "seq_offsets": draw_seq_offsets(jax.random.fold_in(splits[14], 71), 0),
        "tok_counts": draw_tok_counts(jax.random.fold_in(splits[14], 71), 0),
        "norm1_gain": jnp.clip(1.0 + 0.1 * jax.random.normal(splits[5], (D,), jnp.float32), 0.5, 1.5).astype(jnp.bfloat16),
        "norm2_gain": jnp.clip(1.0 + 0.1 * jax.random.normal(splits[6], (D,), jnp.float32), 0.5, 1.5).astype(jnp.bfloat16),
        "w_query": draw_w_query(jax.random.fold_in(splits[14], 71), 0),
        "w_key": draw_w_key(jax.random.fold_in(splits[14], 71), 0),
        "w_value": bell_draw(splits[9], (D, KV_HEADS * HD), D ** -0.5, 0.15625, ((0, 8), (1, 4))),
        "w_out": bell_draw(splits[10], (HEADS * HD, D), (max(HEADS * HD // 64, 1)) ** -0.5, 1.25, ((0, 4), (1, 8))),
        "w_gate": bell_draw(splits[11], (D, FF), D ** -0.5, 0.15625, ((0, 8), (1, 4))),
        "w_up": bell_draw(splits[12], (D, FF), D ** -0.5, 0.15625, ((0, 8), (1, 4))),
        "w_down": bell_draw(splits[13], (FF, D), FF ** -0.5, 0.09375, ((0, 4), (1, 8))),
    }


EPS = 1e-05
THETA = 100000.0
NEG = -1e+30

@jax.custom_vjp
def low(v):
    return lax.optimization_barrier(v.astype(jnp.bfloat16)).astype(jnp.float32)

@jax.custom_vjp
def low_back(v):
    return v

def low_keep(v):
    return (low(v), None)

def low_pass(kept, grad):
    return (grad,)

def back_keep(v):
    return (v, None)

def back_low(kept, grad):
    return (low(grad),)
low.defvjp(low_keep, low_pass)
low_back.defvjp(back_keep, back_low)

def product(left, right):
    return jnp.dot(left, right, precision=lax.Precision.HIGHEST, preferred_element_type=jnp.float32)

def normalize(matrix, gain_vec):
    return matrix * lax.rsqrt(lax.optimization_barrier(jnp.mean(matrix * matrix, axis=1, keepdims=True)) + EPS) * gain_vec[None, :]

def rotary(cosines, sines, matrix):
    count = matrix.shape[0]
    head_count = matrix.shape[1] // HD
    shaped = matrix.reshape(count, head_count, HD)
    first_half = shaped[:, :, :HD // 2]
    second_half = shaped[:, :, HD // 2:]
    cos_rows = cosines[:, None, :]
    sin_rows = sines[:, None, :]
    turned = jnp.concatenate([first_half * cos_rows - second_half * sin_rows, second_half * cos_rows + first_half * sin_rows], axis=2)
    return turned.reshape(count, head_count * HD)

def attend(queries, key_rows, value_rows, offsets, lengths):
    group_rows = queries.shape[0]
    sharing = HEADS // KV_HEADS

    def one_seq(carried, seq_item):
        offset, length = seq_item
        window_start = jnp.minimum(offset, group_rows - MAXLEN).astype(jnp.int32)
        row_index = window_start + jnp.arange(MAXLEN, dtype=jnp.int32)
        member = (row_index >= offset) & (row_index < offset + length)
        allowed = member[:, None] & member[None, :] & (row_index[None, :] <= row_index[:, None])
        q_win = lax.dynamic_slice_in_dim(queries, window_start, MAXLEN, 0).reshape(MAXLEN, KV_HEADS, sharing, HD)
        k_win = lax.dynamic_slice_in_dim(key_rows, window_start, MAXLEN, 0).reshape(MAXLEN, KV_HEADS, HD)
        v_win = lax.dynamic_slice_in_dim(value_rows, window_start, MAXLEN, 0).reshape(MAXLEN, KV_HEADS, HD)
        scores = low_back(HD ** (-0.5) * jnp.einsum('qkgd,tkd->kgqt', q_win, k_win, precision=lax.Precision.HIGHEST))
        scores = jnp.where(allowed[None, None], scores, NEG)
        maximum = lax.optimization_barrier(jnp.max(scores, axis=3, keepdims=True))
        exponent = jnp.exp(scores - maximum)
        probability = low(exponent / lax.optimization_barrier(jnp.sum(exponent, axis=3, keepdims=True)))
        attended = jnp.einsum('kgqt,tkd->qkgd', probability, v_win, precision=lax.Precision.HIGHEST)
        attended = jnp.where(member[:, None], attended.reshape(MAXLEN, HEADS * HD), 0.0)
        earlier = lax.dynamic_slice_in_dim(carried, window_start, MAXLEN, 0)
        return (lax.dynamic_update_slice_in_dim(carried, earlier + attended, window_start, 0), None)
    result, _ = lax.scan(jax.checkpoint(one_seq), jnp.zeros((group_rows, HEADS * HD), jnp.float32), (offsets, lengths))
    return result

def layer(block_rows, live_rows, offsets, lengths, gain_first, gain_second, query_proj, key_proj, value_proj, out_proj, gate_proj, up_proj, down_proj):
    inputs = jnp.where(live_rows[:, None], block_rows, 0.0)
    group_rows = block_rows.shape[0]
    row_index = jnp.arange(group_rows, dtype=jnp.int32)[:, None]
    inside = (row_index >= offsets[None, :]) & (row_index < offsets[None, :] + lengths[None, :])
    position = lax.optimization_barrier(jnp.sum(jnp.where(inside, row_index - offsets[None, :], 0), axis=1)).astype(jnp.float32)
    frequency = THETA ** (-jnp.arange(HD // 2, dtype=jnp.float32) * 2.0 / HD)
    angles = position[:, None] * frequency[None, :]
    cosines = jnp.cos(angles)
    sines = jnp.sin(angles)
    act_first = low(normalize(inputs, gain_first))
    queries = low(rotary(cosines, sines, low_back(product(act_first, query_proj))))
    key_rows = low(rotary(cosines, sines, low_back(product(act_first, key_proj))))
    value_rows = low(low_back(product(act_first, value_proj)))
    head_out = low(low_back(attend(queries, key_rows, value_rows, offsets, lengths)))
    middle = inputs + low_back(product(head_out, out_proj))
    act_second = low(normalize(middle, gain_second))
    gate_val = low_back(product(act_second, gate_proj))
    up_val = low_back(product(act_second, up_proj))
    hidden = low(jax.nn.silu(gate_val) * up_val)
    return middle + low_back(product(hidden, down_proj))

def reference(block_in, cotangent, seq_lengths, seq_offsets, tok_counts, norm1_gain, norm2_gain, w_query, w_key, w_value, w_out, w_gate, w_up, w_down):
    params = tuple((item.astype(jnp.float32) for item in (norm1_gain, norm2_gain, w_query, w_key, w_value, w_out, w_gate, w_up, w_down)))
    inputs = block_in.astype(jnp.float32).reshape(GROUPS, CAP, D)
    upstream = cotangent.astype(jnp.float32).reshape(GROUPS, CAP, D)
    local_rows = jnp.arange(CAP, dtype=jnp.int32)
    owner = local_rows // ROWS
    within = local_rows % ROWS

    def group_step(grad_totals, group_item):
        group_rows, group_cot, lengths, offsets, counts = group_item
        live_rows = within < jnp.take(counts, owner)

        def forward(rows_value, *weights):
            return layer(rows_value, live_rows, offsets, lengths, *weights)
        layer_out, pullback = jax.vjp(forward, group_rows, *params)
        gradients = pullback(group_cot)
        updated = tuple((total + piece for total, piece in zip(grad_totals, gradients[1:])))
        return (updated, (layer_out, gradients[0]))
    zeros = tuple((jnp.zeros(item.shape, jnp.float32) for item in params))
    totals, (outputs, input_grads) = lax.scan(group_step, zeros, (inputs, upstream, seq_lengths, seq_offsets, tok_counts))
    return (outputs.reshape(TOKENS, D).astype(jnp.bfloat16), input_grads.reshape(TOKENS, D), totals[0], totals[1], totals[2], totals[3], totals[4], totals[5], totals[6], totals[7], totals[8])
```

```python
import functools

import jax
import jax.numpy as jnp
import numpy as np
from jax import lax
from jax.experimental import pallas as pl
from jax.experimental.pallas import tpu as pltpu
from jax.sharding import PartitionSpec as P

HD = 96
HALF = 48
PAD = 128
EPS = 1e-05
THETA = 100000.0
NEG = -1e30
LOG2E = 1.4426950408889634
F32 = jnp.float32
BF16 = jnp.bfloat16


PARTNER = [(0, 1), (1, 0), (2, 3), (3, 2)]
PEER = [(0, 2), (2, 0), (1, 3), (3, 1)]

QB = 320
SPANS = (
    (0, 384), (0, 640), (0, 1024), (0, 1280),
    (1024, 640), (1024, 896), (1024, 1280), (1024, 1536),
)


def to_partner(x):
    return lax.ppermute(x, "tensor", PARTNER)


def to_peer(x):
    return lax.ppermute(x, "tensor", PEER)


def nt(a, b):
    return lax.dot_general(a, b, (((1,), (1,)), ((), ())), preferred_element_type=F32)


def tn(a, b):
    return lax.dot_general(a, b, (((0,), (0,)), ((), ())), preferred_element_type=F32)


def nn(a, b):
    return jnp.dot(a, b, preferred_element_type=F32)


def head_spread(sources, width):
    out = np.zeros((width, PAD * len(sources)), np.float32)
    for slot, first in enumerate(sources):
        for lane in range(HALF):
            out[first + lane, slot * PAD + lane] = 1.0
            out[first + HALF + lane, slot * PAD + 64 + lane] = 1.0
    return jnp.asarray(out, BF16)


def params(**kw):
    return pltpu.CompilerParams(vmem_limit_bytes=60 * 2**20, **kw)


def cost(flops, nbytes, trans=0):
    return pl.CostEstimate(flops=int(flops), bytes_accessed=int(nbytes), transcendentals=int(trans))


def qkv_body(order, meta, x0, x1, gain, wp, cos, sin, *rest):
    act_out, qkv_out = rest[-2:]
    step = pl.program_id(0)
    bm = x0.shape[0]
    x = jnp.where(step < 2, x0[...], x1[...]).astype(F32)
    row = order[step] * bm + lax.broadcasted_iota(jnp.int32, (bm, 1), 0)
    x = jnp.where(row < meta[1], x, 0.0)
    factor = lax.rsqrt(jnp.mean(x * x, axis=1, keepdims=True) + EPS)
    act = (x * factor * gain[...]).astype(BF16)
    act_out[...] = act
    y = nn(act, wp[...])
    c, s = cos[...], sin[...]
    for slot in range(8):
        part = y[:, slot * PAD : (slot + 1) * PAD]
        if slot % 4 != 3:
            part = part * c + pltpu.roll(part, 64, 1) * s
        qkv_out[:, slot * PAD : (slot + 1) * PAD] = part.astype(BF16)


def qkv_call(order, meta, x0, x1, gain, wp, cos, sin, earlier):
    rows, d = x0.shape
    bm = rows // 2
    total = rows * 4
    specs = [
        pl.BlockSpec((bm, d), lambda i, o, m: (jnp.minimum(i, 1), 0)),
        pl.BlockSpec((bm, d), lambda i, o, m: (jnp.maximum(i - 2, 0), 0)),
        pl.BlockSpec((1, d), lambda i, o, m: (0, 0)),
        pl.BlockSpec(wp.shape, lambda i, o, m: (0, 0)),
        pl.BlockSpec((bm, PAD), lambda i, o, m: (o[i], 0)),
        pl.BlockSpec((bm, PAD), lambda i, o, m: (o[i], 0)),
    ]
    args = [order, meta, x0, x1, gain, wp, cos, sin]
    alias = {}
    if earlier is not None:
        specs += [pl.BlockSpec(memory_space=pl.ANY)] * 2
        alias = {8: 0, 9: 1}
        args += list(earlier)
    return pl.pallas_call(
        qkv_body,
        grid_spec=pltpu.PrefetchScalarGridSpec(
            num_scalar_prefetch=2,
            grid=(4,),
            in_specs=specs,
            out_specs=[
                pl.BlockSpec((bm, d), lambda i, o, m: (o[i], 0)),
                pl.BlockSpec((bm, 8 * PAD), lambda i, o, m: (o[i], 0)),
            ],
        ),
        out_shape=[
            jax.ShapeDtypeStruct((total, d), BF16),
            jax.ShapeDtypeStruct((total, 8 * PAD), BF16),
        ],
        input_output_aliases=alias,
        compiler_params=params(),
        cost_estimate=cost(2 * 2 * rows * d * 8 * PAD, 2 * rows * (4 * d + 16 * PAD) + wp.size * 2),
        name="qkv_proj",
    )(*args)


def score_mask(index, start, width, len0):
    first_row = index * QB
    rows = first_row + lax.broadcasted_iota(jnp.int32, (QB, 1), 0)
    begin = jnp.where(rows >= len0, len0, 0)

    def mask(col, cols):
        keys = start + col + lax.broadcasted_iota(jnp.int32, (QB, cols), 1)
        return (keys <= rows) & (keys >= begin)

    return mask


def masked_scores(q2, keys, index, start, width, len0):
    s = nt(q2, keys)
    mask = score_mask(index, start, width, len0)
    causal_from = ((index * QB - start) // PAD) * PAD
    if index == 3:
        pieces = [(0, width, True)]
    elif index < 3:
        pieces = [(0, causal_from, False), (causal_from, width - causal_from, True)]
    elif causal_from <= 256:
        pieces = [(0, width, True)]
    else:
        pieces = [(0, 256, True), (256, causal_from - 256, False), (causal_from, width - causal_from, True)]
    halves = []
    for head in range(2):
        sh = s[head * QB : (head + 1) * QB]
        cols = []
        for col, n, masked in pieces:
            if n <= 0:
                continue
            part = sh[:, col : col + n]
            cols.append(jnp.where(mask(col, n), part, NEG) if masked else part)
        halves.append(cols[0] if len(cols) == 1 else jnp.concatenate(cols, axis=1))
    return halves


def attn_fwd_body(order, meta, q_ref, kv_ref, wo_ref, *rest):
    o_ref, lse_ref, part_ref, o_acc = rest[-4:]
    step = pl.program_id(0)
    kvh = pl.program_id(1)
    index = order[step]
    scale = HD ** (-0.5)

    def block(i):
        start, width = SPANS[i]
        q2 = jnp.concatenate([q_ref[:, :PAD], q_ref[:, PAD:]], axis=0)
        keys = kv_ref[start : start + width, :PAD]
        values = kv_ref[start : start + width, PAD:]
        halves = masked_scores(q2, keys, i, start, width, meta[0])
        alive = i * QB + lax.broadcasted_iota(jnp.int32, (QB, 1), 0) < meta[1]
        for head in range(2):
            s = halves[head]
            top = jnp.max(s, axis=1, keepdims=True)
            e = jnp.exp2((s - top) * (scale * LOG2E))
            total = jnp.sum(e, axis=1, keepdims=True)
            p = (e * (1.0 / total)).astype(BF16)
            out = nn(p, values)
            o_acc[kvh * 2 + head] = jnp.where(alive, out, 0.0).astype(BF16)
            lse = top * (scale * LOG2E) + jnp.log2(total)
            lse_ref[:, head * 64 : (head + 1) * 64] = jnp.broadcast_to(lse, (QB, 64))

    for i in range(8):
        pl.when(index == i)(functools.partial(block, i))

    @pl.when(kvh == 1)
    def _():
        o = jnp.concatenate([o_acc[h] for h in range(4)], axis=1)
        o_ref[...] = o
        part_ref[...] = nt(o, wo_ref[...]).astype(BF16)


def attn_fwd_call(order, meta, qkv, wop, earlier):
    total, _ = qkv.shape
    d = wop.shape[0]
    specs = [
        pl.BlockSpec((QB, 2 * PAD), lambda i, h, o, m: (o[i], 2 * h)),
        pl.BlockSpec((total, 2 * PAD), lambda i, h, o, m: (0, 2 * h + 1)),
        pl.BlockSpec(wop.shape, lambda i, h, o, m: (0, 0)),
    ]
    args = [order, meta, qkv, qkv, wop]
    alias = {}
    if earlier is not None:
        specs += [pl.BlockSpec(memory_space=pl.ANY)] * 2
        alias = {5: 0, 6: 1}
        args += list(earlier)
    return pl.pallas_call(
        attn_fwd_body,
        grid_spec=pltpu.PrefetchScalarGridSpec(
            num_scalar_prefetch=2,
            grid=(4, 2),
            in_specs=specs,
            out_specs=[
                pl.BlockSpec((QB, 4 * PAD), lambda i, h, o, m: (o[i], 0)),
                pl.BlockSpec((QB, PAD), lambda i, h, o, m: (o[i], h)),
                pl.BlockSpec((QB, d), lambda i, h, o, m: (i, 0)),
            ],
            scratch_shapes=[pltpu.VMEM((4, QB, PAD), BF16)],
        ),
        out_shape=[
            jax.ShapeDtypeStruct((total, 4 * PAD), BF16),
            jax.ShapeDtypeStruct((total, 2 * PAD), F32),
            jax.ShapeDtypeStruct((total // 2, d), BF16),
        ],
        input_output_aliases=alias,
        compiler_params=params(),
        cost_estimate=cost(9e9, 12e6, 5e6),
        name="attn_fwd",
    )(*args)


def attn_bwd_body(meta, q_ref, kv_ref, do_ref, lse_ref, cos, sin, cos_all, sin_all, out_ref, dk_acc, dv_acc):
    step = pl.program_id(1)
    scale = HD ** (-0.5)

    @pl.when(step == 0)
    def _():
        dk_acc[...] = jnp.zeros_like(dk_acc)
        dv_acc[...] = jnp.zeros_like(dv_acc)

    def block(i):
        start, width = SPANS[i]
        q2 = jnp.concatenate([q_ref[:, :PAD], q_ref[:, PAD:]], axis=0)
        do2 = jnp.concatenate([do_ref[:, :PAD], do_ref[:, PAD:]], axis=0)
        keys = kv_ref[start : start + width, :PAD]
        values = kv_ref[start : start + width, PAD:]
        halves = masked_scores(q2, keys, i, start, width, meta[0])
        dp2 = nt(do2, values)
        ps, dss = [], []
        for head in range(2):
            lse = lse_ref[:, head * 64 : head * 64 + 1]
            p = jnp.exp2(halves[head] * (scale * LOG2E) - lse)
            dp = dp2[head * QB : (head + 1) * QB]
            delta = jnp.sum(p * dp, axis=1, keepdims=True)
            dss.append((p * (dp - delta)).astype(BF16))
            ps.append(p.astype(BF16))
        pb = jnp.concatenate(ps, axis=0)
        ds = jnp.concatenate(dss, axis=0)
        dv_acc[start : start + width, :] += tn(pb, do2)
        dk_acc[start : start + width, :] += tn(ds, q2)
        dq = nn(ds, keys) * scale
        c, s = cos[...], sin[...]
        for head in range(2):
            part = dq[head * QB : (head + 1) * QB]
            part = part * c - pltpu.roll(part, 64, 1) * s
            out_ref[i * QB : (i + 1) * QB, head * PAD : (head + 1) * PAD] = part.astype(BF16)

    for i in range(8):
        pl.when(step == i)(functools.partial(block, i))

    @pl.when(step == 7)
    def _():
        dk = dk_acc[...] * scale
        dk = dk * cos_all[...] - pltpu.roll(dk, 64, 1) * sin_all[...]
        out_ref[:, 2 * PAD : 3 * PAD] = dk.astype(BF16)
        out_ref[:, 3 * PAD : 4 * PAD] = dv_acc[...].astype(BF16)


def attn_bwd_call(meta, qkv, dheads, lse, cos, sin):
    total, _ = qkv.shape
    return pl.pallas_call(
        attn_bwd_body,
        grid_spec=pltpu.PrefetchScalarGridSpec(
            num_scalar_prefetch=1,
            grid=(2, 8),
            in_specs=[
                pl.BlockSpec((QB, 2 * PAD), lambda h, i, m: (i, 2 * h)),
                pl.BlockSpec((total, 2 * PAD), lambda h, i, m: (0, 2 * h + 1)),
                pl.BlockSpec((QB, 2 * PAD), lambda h, i, m: (i, h)),
                pl.BlockSpec((QB, PAD), lambda h, i, m: (i, h)),
                pl.BlockSpec((QB, PAD), lambda h, i, m: (i, 0)),
                pl.BlockSpec((QB, PAD), lambda h, i, m: (i, 0)),
                pl.BlockSpec((total, PAD), lambda h, i, m: (0, 0)),
                pl.BlockSpec((total, PAD), lambda h, i, m: (0, 0)),
            ],
            out_specs=pl.BlockSpec((total, 4 * PAD), lambda h, i, m: (0, h)),
            scratch_shapes=[pltpu.VMEM((total, PAD), F32), pltpu.VMEM((total, PAD), F32)],
        ),
        out_shape=jax.ShapeDtypeStruct((total, 8 * PAD), BF16),
        compiler_params=params(),
        cost_estimate=cost(30e9, 25e6, 10e6),
        name="attn_bwd",
    )(meta, qkv, qkv, dheads, lse, cos, sin, cos, sin)


def mlp_body(a0, a1, c0, c1, w_ref, hid_out, dg_out, du_out, mo_out, da_out):
    first = pl.program_id(0) < pl.num_programs(0) // 2
    act = jnp.where(first, a0[...], a1[...])
    cot = jnp.where(first, c0[...], c1[...])
    ff = w_ref.shape[1] // 3
    wg, wu, wd = w_ref[:, :ff], w_ref[:, ff : 2 * ff], w_ref[:, 2 * ff :]
    gate = nn(act, wg)
    up = nn(act, wu)
    dh = nn(cot, wd)
    sig = 1.0 / (1.0 + jnp.exp(-gate))
    gs = gate * sig
    hid = (gs * up).astype(BF16)
    dg = (dh * up * sig * (1.0 + gate * (1.0 - sig))).astype(BF16)
    du = (dh * gs).astype(BF16)
    hid_out[...] = hid
    dg_out[...] = dg
    du_out[...] = du
    mo_out[...] = nt(hid, wd).astype(BF16)
    da_out[...] = (nt(dg, wg) + nt(du, wu)).astype(BF16)


def mlp_call(a0, a1, c0, c1, w):
    rows, d = a0.shape
    ff = w.shape[1] // 3
    parts = 2
    bm = rows // parts
    lo = lambda i: (jnp.minimum(i, parts - 1), 0)
    hi = lambda i: (jnp.maximum(i - parts, 0), 0)
    return pl.pallas_call(
        mlp_body,
        grid=(2 * parts,),
        in_specs=[
            pl.BlockSpec((bm, d), lo),
            pl.BlockSpec((bm, d), hi),
            pl.BlockSpec((bm, d), lo),
            pl.BlockSpec((bm, d), hi),
            pl.BlockSpec(w.shape, lambda i: (0, 0), pipeline_mode=pl.Buffered(1)),
        ],
        out_specs=[pl.BlockSpec((bm, ff), lambda i: (i, 0))] * 3
        + [pl.BlockSpec((bm, d), lambda i: (i, 0))] * 2,
        out_shape=[jax.ShapeDtypeStruct((2 * rows, ff), BF16)] * 3
        + [jax.ShapeDtypeStruct((2 * rows, d), BF16)] * 2,
        compiler_params=params(),
        cost_estimate=cost(12 * 2 * rows * d * ff, 2 * rows * (8 * d + 6 * ff) + w.size * 2, 2 * rows * ff),
        name="mlp_both",
    )(a0, a1, c0, c1, w)


def mlp_grad_body(a0, a1, a2, a3, c0, c1, c2, c3, h0, h1, g0, g1, u0, u1, out):
    step = pl.program_id(0)
    per = pl.num_programs(0) // 3
    rows = a0.shape[0]

    def total(left, lo, hi):
        acc = tn(left[0][...], lo[:rows])
        acc = acc + tn(left[1][...], lo[rows:])
        acc = acc + tn(left[2][...], hi[:rows])
        acc = acc + tn(left[3][...], hi[rows:])
        out[...] = acc.astype(BF16)

    acts, cots = (a0, a1, a2, a3), (c0, c1, c2, c3)

    @pl.when(step < per)
    def _():
        total(acts, g0, g1)

    @pl.when((step >= per) & (step < 2 * per))
    def _():
        total(acts, u0, u1)

    @pl.when(step >= 2 * per)
    def _():
        total(cots, h0, h1)


def mlp_grad_call(acts, cots, hid, dg, du):
    rows, d = acts[0].shape
    ff = hid[0].shape[1]
    per = 4
    bn = ff // per
    whole = pl.BlockSpec((rows, d), lambda i: (0, 0), pipeline_mode=pl.Buffered(1))

    def part(k):
        return pl.BlockSpec((2 * rows, bn), lambda i: (0, jnp.clip(i - k * per, 0, per - 1)))

    return pl.pallas_call(
        mlp_grad_body,
        grid=(3 * per,),
        in_specs=[whole] * 8 + [part(2)] * 2 + [part(0)] * 2 + [part(1)] * 2,
        out_specs=pl.BlockSpec((d, bn), lambda i: (0, i)),
        out_shape=jax.ShapeDtypeStruct((d, 3 * ff), BF16),
        compiler_params=params(),
        cost_estimate=cost(6 * 4 * rows * d * ff, 16 * rows * d + 24 * rows * ff + 6 * d * ff),
        name="mlp_grad",
    )(*acts, *cots, *hid, *dg, *du)


def heads_grad_body(order, meta, d0, d1, d2, d3, o_ref, wo_ref, un_ref, dh_out, g_out, acc):
    step = pl.program_id(0)

    def piece(ref, first):
        dmid = ref[...]
        rows = dmid.shape[0]
        row = order[step] * rows + lax.broadcasted_iota(jnp.int32, (rows, 1), 0)
        dh = nn(dmid, wo_ref[...])
        dh_out[...] = jnp.where(row < meta[1], dh, 0.0).astype(BF16)
        g = tn(dmid, o_ref[...])
        if first:
            acc[...] = g
        else:
            acc[...] += g

    for k, ref in enumerate((d0, d1, d2, d3)):
        pl.when(step == k)(functools.partial(piece, ref, k == 0))

    @pl.when(step == 3)
    def _():
        g_out[...] = nt(acc[...].astype(BF16), un_ref[...]).astype(BF16)


def heads_grad_call(order, meta, pieces, o, wop, spread):
    rows, d = pieces[0].shape
    hw = o.shape[1]
    whole = pl.BlockSpec((rows, d), lambda i, o, m: (0, 0))
    return pl.pallas_call(
        heads_grad_body,
        grid_spec=pltpu.PrefetchScalarGridSpec(
            num_scalar_prefetch=2,
            grid=(4,),
            in_specs=[whole] * 4
            + [
                pl.BlockSpec((rows, hw), lambda i, o, m: (o[i], 0)),
                pl.BlockSpec(wop.shape, lambda i, o, m: (0, 0)),
                pl.BlockSpec(spread.shape, lambda i, o, m: (0, 0)),
            ],
            out_specs=[
                pl.BlockSpec((rows, hw), lambda i, o, m: (o[i], 0)),
                pl.BlockSpec((d, spread.shape[0]), lambda i, o, m: (0, 0)),
            ],
            scratch_shapes=[pltpu.VMEM((d, hw), F32)],
        ),
        out_shape=[
            jax.ShapeDtypeStruct((4 * rows, hw), BF16),
            jax.ShapeDtypeStruct((d, spread.shape[0]), BF16),
        ],
        compiler_params=params(),
        cost_estimate=cost(4 * 4 * rows * d * hw, 8 * rows * d + 16 * rows * hw + 4 * d * hw),
        name="heads_grad",
    )(order, meta, *pieces, o, wop, spread)


def act1_grad_body(order, g_ref, w_ref, out):
    out[...] = nt(g_ref[...], w_ref[...]).astype(BF16)


def act1_grad_call(order, dqkv, wp):
    total, width = dqkv.shape
    d = wp.shape[0]
    rows = total // 8
    return pl.pallas_call(
        act1_grad_body,
        grid_spec=pltpu.PrefetchScalarGridSpec(
            num_scalar_prefetch=1,
            grid=(8,),
            in_specs=[
                pl.BlockSpec((rows, width), lambda i, o: (o[i], 0)),
                pl.BlockSpec(wp.shape, lambda i, o: (0, 0)),
            ],
            out_specs=pl.BlockSpec((rows, d), lambda i, o: (i, 0)),
        ),
        out_shape=jax.ShapeDtypeStruct((total, d), BF16),
        compiler_params=params(),
        cost_estimate=cost(2 * total * width * d, 2 * total * (width + d)),
        name="act1_grad",
    )(order, dqkv, wp)


def qkv_grad_body(a_ref, g_ref, un_ref, out):
    g = tn(a_ref[...], g_ref[...]).astype(BF16)
    out[...] = nt(g, un_ref[...]).astype(BF16)


def qkv_grad_call(act, dqkv, spread):
    total, d = act.shape
    bd = 256
    return pl.pallas_call(
        qkv_grad_body,
        grid=(d // bd,),
        in_specs=[
            pl.BlockSpec((total, bd), lambda i: (0, i)),
            pl.BlockSpec(dqkv.shape, lambda i: (0, 0), pipeline_mode=pl.Buffered(1)),
            pl.BlockSpec(spread.shape, lambda i: (0, 0), pipeline_mode=pl.Buffered(1)),
        ],
        out_specs=pl.BlockSpec((bd, spread.shape[0]), lambda i: (i, 0)),
        out_shape=jax.ShapeDtypeStruct((d, spread.shape[0]), BF16),
        compiler_params=params(),
        cost_estimate=cost(2 * total * d * 8 * PAD, 2 * total * (d + 8 * PAD)),
        name="qkv_grad",
    )(act, dqkv, spread)


def on_device(
    block_in, cotangent, seq_lengths, seq_offsets, tok_counts, norm1_gain, norm2_gain,
    w_query, w_key, w_value, w_out, w_gate, w_up, w_down,
):
    rows, d = block_in.shape
    group_rows = rows * 4
    me = lax.axis_index("tensor")
    core, chip = me % 2, me // 2
    qc, kc = w_query.shape[1], w_key.shape[1]
    ff = w_gate.shape[1]

    near = jnp.stack([me, me ^ 1, me ^ 2, me ^ 3]).astype(jnp.int32)
    half_blocks = (near[:, None] * 2 + jnp.arange(2, dtype=jnp.int32)[None, :]).reshape(8)
    len0 = seq_lengths[0, 0]
    total = seq_lengths[0, 0] + seq_lengths[0, 1]
    meta = jnp.stack([len0, total]).astype(jnp.int32)

    gains = jnp.pad(jnp.stack([norm1_gain, norm2_gain], axis=1), ((0, 0), (0, PAD - 2)))
    w_first = jnp.concatenate([w_query, w_key, w_value, w_out.T, gains], axis=1)
    w_second = jnp.concatenate([w_gate, w_up, w_down.T], axis=1)
    first_all = lax.all_gather(w_first, "dp", axis=0, tiled=True)
    second_all = lax.all_gather(w_second, "dp", axis=0, tiled=True)
    x_peer = to_peer(block_in)
    x_partner = to_partner(block_in)
    x_diag = to_partner(x_peer)
    cot_peer = to_peer(cotangent)
    cot_partner = to_partner(cotangent)
    cot_diag = to_partner(cot_peer)

    qw = 4 * HD
    kw = 2 * HD
    spread_qkv = head_spread(
        [0, HD, qw, qw + kw, 2 * HD, 3 * HD, qw + HD, qw + kw + HD], qw + 2 * kw
    )
    spread_o = head_spread([0, HD, 2 * HD, 3 * HD], qw)
    wp = nn(first_all[:, : qc + 2 * kc], spread_qkv).astype(BF16)
    wop = nn(first_all[:, qc + 2 * kc : 2 * qc + 2 * kc], spread_o).astype(BF16)
    gain_cols = first_all[:, 2 * qc + 2 * kc : 2 * qc + 2 * kc + 2].astype(F32)
    gain1 = gain_cols[:, 0][None, :]
    gain2 = gain_cols[:, 1][None, :]

    row_index = jnp.arange(group_rows, dtype=jnp.int32)
    position = jnp.where(
        row_index < len0, row_index, jnp.where(row_index < total, row_index - len0, 0)
    ).astype(F32)
    frequency = THETA ** (-jnp.arange(HALF, dtype=F32) * 2.0 / HD)
    angles = position[:, None] * frequency[None, :]
    cosines, sines = jnp.cos(angles), jnp.sin(angles)
    gap = jnp.zeros((group_rows, 64 - HALF), F32)
    cos = jnp.concatenate([cosines, gap, cosines, gap], axis=1)
    sin = jnp.concatenate([-sines, gap, sines, gap], axis=1)

    earlier = qkv_call(half_blocks[:4], meta, block_in, x_partner, gain1, wp, cos, sin, None)
    act1, qkv = qkv_call(half_blocks[4:], meta, x_peer, x_diag, gain1, wp, cos, sin, earlier)
    o_first, lse_first, part_peer = attn_fwd_call(half_blocks[4:], meta, qkv, wop, None)
    o_all, lse, part_own = attn_fwd_call(half_blocks[:4], meta, qkv, wop, (o_first, lse_first))
    from_partner = to_partner(part_peer[rows:])
    chip_sum = (part_peer[:rows].astype(F32) + from_partner.astype(F32)).astype(BF16)
    attn_peer = to_peer(chip_sum)
    attn_partner = to_partner(part_own[rows:])

    row_live = (me * rows + jnp.arange(rows, dtype=jnp.int32) < total)[:, None]
    xin = jnp.where(row_live, block_in.astype(F32), 0.0)
    mid = xin + (part_own[:rows].astype(F32) + attn_partner.astype(F32) + attn_peer.astype(F32))
    factor2 = lax.rsqrt(jnp.mean(mid * mid, axis=1, keepdims=True) + EPS)
    act2 = (mid * factor2 * gain2).astype(BF16)
    act2_peer = to_peer(act2)
    act2_partner = to_partner(act2)
    act2_diag = to_partner(act2_peer)

    hid_a, dg_a, du_a, mo_a, da_a = mlp_call(act2, act2_partner, cotangent, cot_partner, second_all)
    hid_b, dg_b, du_b, mo_b, da_b = mlp_call(act2_peer, act2_diag, cot_peer, cot_diag, second_all)

    da_in = to_partner(da_b[rows:])
    da_sum = (da_b[:rows].astype(F32) + da_in.astype(F32)).astype(BF16)
    da_peer = to_peer(da_sum)
    da_partner = to_partner(da_a[rows:])
    dact2 = da_a[:rows].astype(F32) + da_partner.astype(F32) + da_peer.astype(F32)
    normed2 = mid * factor2
    dn2 = dact2 * gain2
    inner2 = jnp.mean(dn2 * normed2, axis=1, keepdims=True)
    dmid = cotangent.astype(F32) + factor2 * (dn2 - normed2 * inner2)
    dmid_low = dmid.astype(BF16)
    dmid_peer = to_peer(dmid_low)
    dmid_partner = to_partner(dmid_low)
    dmid_diag = to_partner(dmid_peer)

    g_second = mlp_grad_call(
        (act2, act2_partner, act2_peer, act2_diag),
        (cotangent, cot_partner, cot_peer, cot_diag),
        (hid_a, hid_b), (dg_a, dg_b), (du_a, du_b),
    )
    g_second = lax.psum_scatter(g_second, "dp", scatter_dimension=0, tiled=True)

    mo_in = to_partner(mo_b[rows:])
    mo_sum = (mo_b[:rows].astype(F32) + mo_in.astype(F32)).astype(BF16)
    mo_peer = to_peer(mo_sum)
    mo_partner = to_partner(mo_a[rows:])
    block_out = (
        mid + (mo_a[:rows].astype(F32) + mo_partner.astype(F32) + mo_peer.astype(F32))
    ).astype(BF16)

    dheads, g_out = heads_grad_call(
        near, meta, (dmid_low, dmid_partner, dmid_peer, dmid_diag), o_all, wop, spread_o
    )
    dqkv = attn_bwd_call(meta, qkv, dheads, lse, cos, sin)
    back_order = jnp.concatenate([half_blocks[4:], half_blocks[2:4], half_blocks[:2]])
    back = act1_grad_call(back_order, dqkv, wp)
    back_in = to_partner(back[rows : 2 * rows])
    back_sum = (back[:rows].astype(F32) + back_in.astype(F32)).astype(BF16)
    back_peer = to_peer(back_sum)
    back_partner = to_partner(back[2 * rows : 3 * rows])
    g_qkv = qkv_grad_call(act1, dqkv, spread_qkv)
    g_first = lax.psum_scatter(
        jnp.concatenate([g_qkv, g_out], axis=1), "dp", scatter_dimension=0, tiled=True
    )

    dact1 = back[3 * rows :].astype(F32) + back_partner.astype(F32) + back_peer.astype(F32)
    factor1 = lax.rsqrt(jnp.mean(xin * xin, axis=1, keepdims=True) + EPS)
    normed1 = xin * factor1
    dn1 = dact1 * gain1
    inner1 = jnp.mean(dn1 * normed1, axis=1, keepdims=True)
    grad_input = jnp.where(row_live, dmid + factor1 * (dn1 - normed1 * inner1), 0.0)

    g_first = g_first.astype(F32)
    g_second = g_second.astype(F32)
    g_q, g_k = g_first[:, :qc], g_first[:, qc : qc + kc]
    g_v, g_o = g_first[:, qc + kc : qc + 2 * kc], g_first[:, qc + 2 * kc :]
    g_gate, g_up, g_down = g_second[:, :ff], g_second[:, ff : 2 * ff], g_second[:, 2 * ff :]
    dot1 = jnp.sum(g_first[:, : qc + 2 * kc] * w_first[:, : qc + 2 * kc].astype(F32), axis=1)
    dot2 = jnp.sum(g_second[:, : 2 * ff] * w_second[:, : 2 * ff].astype(F32), axis=1)
    dots = lax.psum(jnp.stack([dot1, dot2]), "tensor")
    return (
        block_out,
        grad_input,
        dots[0] / norm1_gain.astype(F32),
        dots[1] / norm2_gain.astype(F32),
        g_q,
        g_k,
        g_v,
        g_o.T,
        g_gate,
        g_up,
        g_down.T,
    )


def solution(mesh):
    in_specs = (
        P(("dp", "tensor"), None),
        P(("dp", "tensor"), None),
        P("dp", None),
        P("dp", None),
        P("dp", "tensor"),
        P("dp"),
        P("dp"),
        P("dp", "tensor"),
        P("dp", "tensor"),
        P("dp", "tensor"),
        P("tensor", "dp"),
        P("dp", "tensor"),
        P("dp", "tensor"),
        P("tensor", "dp"),
    )
    out_specs = (
        P(("dp", "tensor"), None),
        P(("dp", "tensor"), None),
        P("dp"),
        P("dp"),
        P("dp", "tensor"),
        P("dp", "tensor"),
        P("dp", "tensor"),
        P("tensor", "dp"),
        P("dp", "tensor"),
        P("dp", "tensor"),
        P("tensor", "dp"),
    )
    return jax.shard_map(
        on_device, mesh=mesh, in_specs=in_specs, out_specs=out_specs, check_vma=False
    )
```

```python
import functools

import jax
import jax.numpy as jnp
import numpy as np
from jax import lax
from jax.experimental import pallas as pl
from jax.experimental.pallas import tpu as pltpu
from jax.sharding import PartitionSpec as P


HD = 96
HALF = 48
PAD = 128
EPS = 1e-05
THETA = 100000.0
NEG = -1e30
LOG2E = 1.4426950408889634
F32 = jnp.float32
BF16 = jnp.bfloat16


PARTNER = [(0, 1), (1, 0), (2, 3), (3, 2)]
PEER = [(0, 2), (2, 0), (1, 3), (3, 1)]

QB = 320
SPANS = (
    (0, 384), (0, 640), (0, 1024), (0, 1280),
    (1024, 640), (1024, 896), (1024, 1280), (1024, 1536),
)


def to_partner(x):
    return lax.ppermute(x, "tensor", PARTNER)


def to_peer(x):
    return lax.ppermute(x, "tensor", PEER)


def across(x):
    n = lax.axis_size("dp")
    return lax.ppermute(x, "dp", [(i, i ^ 1) for i in range(n)])


def along(x, shift):
    n = lax.axis_size("dp")
    return lax.ppermute(x, "dp", [(i, (i + 2 * shift) % n) for i in range(n)])


def gather_pieces(x):
    n = lax.axis_size("dp") // 2
    mine, other = [x], [across(x)]
    for _ in range(1, n):
        mine.append(along(mine[-1], 1))
        other.append(across(mine[-1]))
    return [piece for pair in zip(mine, other) for piece in pair]


def reduce_pieces(mine, theirs):
    n = lax.axis_size("dp") // 2
    rows = mine.shape[0] // n
    came = across(theirs)
    sums = [
        mine[k * rows : (k + 1) * rows].astype(F32) + came[k * rows : (k + 1) * rows].astype(F32)
        for k in range(n)
    ]
    arrived = [along(sums[k].astype(BF16), k) for k in range(1, n)]
    total = sums[0]
    for piece in arrived:
        total = total + piece.astype(F32)
    return total


def pair_split(g, where, mine_ref, theirs_ref):
    pairs = lax.axis_size("dp") // 2
    rows = g.shape[0] // (2 * pairs)
    even = where[0] == 0
    for k in range(pairs):
        first = g[2 * k * rows : (2 * k + 1) * rows]
        second = g[(2 * k + 1) * rows : (2 * k + 2) * rows]
        slot = lax.rem(k - where[1] + pairs, pairs)
        at = pl.ds(pl.multiple_of(slot * rows, rows), rows)
        mine_ref[at, :] = jnp.where(even, first, second).astype(BF16)
        theirs_ref[at, :] = jnp.where(even, second, first).astype(BF16)


def nt(a, b):
    return lax.dot_general(a, b, (((1,), (1,)), ((), ())), preferred_element_type=F32)


def tn(a, b):
    return lax.dot_general(a, b, (((0,), (0,)), ((), ())), preferred_element_type=F32)


def nn(a, b):
    return jnp.dot(a, b, preferred_element_type=F32)


def head_spread(sources, width):
    out = np.zeros((width, PAD * len(sources)), np.float32)
    for slot, first in enumerate(sources):
        for lane in range(HALF):
            out[first + lane, slot * PAD + lane] = 1.0
            out[first + HALF + lane, slot * PAD + 64 + lane] = 1.0
    return jnp.asarray(out, BF16)


def params(**kw):
    return pltpu.CompilerParams(vmem_limit_bytes=60 * 2**20, **kw)


def cost(flops, nbytes, trans=0):
    return pl.CostEstimate(flops=int(flops), bytes_accessed=int(nbytes), transcendentals=int(trans))


def prep_body(pieces, width, order, *refs):
    spread, spread_o, eye = refs[pieces : pieces + 3]
    wp_out, wo_out, gain_out = refs[pieces + 3 :]

    def place(ref):
        wp_out[...] = nn(ref[:, :width], spread[...]).astype(BF16)
        wo_out[...] = nn(ref[:, width : width + spread_o.shape[0]], spread_o[...]).astype(BF16)
        gain_out[0] = tn(ref[:, width + spread_o.shape[0] :], eye[...])[:8]

    for k in range(pieces):
        pl.when(pl.program_id(0) == k)(functools.partial(place, refs[k]))


def prep_call(order, pieces, spread, spread_o):
    rows, _ = pieces[0].shape
    n = len(pieces)
    eye = jnp.eye(rows, dtype=BF16)
    whole = lambda a: pl.BlockSpec(a.shape, lambda i, o: (0, 0))
    return pl.pallas_call(
        functools.partial(prep_body, n, spread.shape[0]),
        grid_spec=pltpu.PrefetchScalarGridSpec(
            num_scalar_prefetch=1,
            grid=(n,),
            in_specs=[whole(a) for a in (*pieces, spread, spread_o, eye)],
            out_specs=[
                pl.BlockSpec((rows, spread.shape[1]), lambda i, o: (o[i], 0)),
                pl.BlockSpec((rows, spread_o.shape[1]), lambda i, o: (o[i], 0)),
                pl.BlockSpec((1, 8, rows), lambda i, o: (o[i], 0, 0)),
            ],
        ),
        out_shape=[
            jax.ShapeDtypeStruct((n * rows, spread.shape[1]), BF16),
            jax.ShapeDtypeStruct((n * rows, spread_o.shape[1]), BF16),
            jax.ShapeDtypeStruct((n, 8, rows), F32),
        ],
        compiler_params=params(),
        cost_estimate=cost(4e9, 9e6),
        name="weights_prep",
    )(order, *pieces, spread, spread_o, eye)


def qkv_body(order, meta, x0, x1, gain, wp, cos, sin, *rest):
    act_out, qkv_out = rest[-2:]
    step = pl.program_id(0)
    bm = x0.shape[0]
    x = jnp.where(step < 2, x0[...], x1[...]).astype(F32)
    row = order[step] * bm + lax.broadcasted_iota(jnp.int32, (bm, 1), 0)
    x = jnp.where(row < meta[1], x, 0.0)
    factor = lax.rsqrt(jnp.mean(x * x, axis=1, keepdims=True) + EPS)
    act = (x * factor * gain[...]).astype(BF16)
    act_out[...] = act
    y = nn(act, wp[...])
    c, s = cos[...], sin[...]
    for slot in range(8):
        part = y[:, slot * PAD : (slot + 1) * PAD]
        if slot % 4 != 3:
            part = part * c + pltpu.roll(part, 64, 1) * s
        qkv_out[:, slot * PAD : (slot + 1) * PAD] = part.astype(BF16)


def qkv_call(order, meta, x0, x1, gain, wp, cos, sin, earlier):
    rows, d = x0.shape
    bm = rows // 2
    total = rows * 4
    specs = [
        pl.BlockSpec((bm, d), lambda i, o, m: (jnp.minimum(i, 1), 0)),
        pl.BlockSpec((bm, d), lambda i, o, m: (jnp.maximum(i - 2, 0), 0)),
        pl.BlockSpec((1, d), lambda i, o, m: (0, 0)),
        pl.BlockSpec(wp.shape, lambda i, o, m: (0, 0)),
        pl.BlockSpec((bm, PAD), lambda i, o, m: (o[i], 0)),
        pl.BlockSpec((bm, PAD), lambda i, o, m: (o[i], 0)),
    ]
    args = [order, meta, x0, x1, gain, wp, cos, sin]
    alias = {}
    if earlier is not None:
        specs += [pl.BlockSpec(memory_space=pl.ANY)] * 2
        alias = {8: 0, 9: 1}
        args += list(earlier)
    return pl.pallas_call(
        qkv_body,
        grid_spec=pltpu.PrefetchScalarGridSpec(
            num_scalar_prefetch=2,
            grid=(4,),
            in_specs=specs,
            out_specs=[
                pl.BlockSpec((bm, d), lambda i, o, m: (o[i], 0)),
                pl.BlockSpec((bm, 8 * PAD), lambda i, o, m: (o[i], 0)),
            ],
        ),
        out_shape=[
            jax.ShapeDtypeStruct((total, d), BF16),
            jax.ShapeDtypeStruct((total, 8 * PAD), BF16),
        ],
        input_output_aliases=alias,
        compiler_params=params(),
        cost_estimate=cost(2 * 2 * rows * d * 8 * PAD, 2 * rows * (4 * d + 16 * PAD) + wp.size * 2),
        name="qkv_proj",
    )(*args)


def score_mask(index, start, len0):
    first_row = index * QB
    rows = first_row + lax.broadcasted_iota(jnp.int32, (QB, 1), 0)
    begin = jnp.where(rows >= len0, len0, 0)

    def mask(col, cols):
        keys = start + col + lax.broadcasted_iota(jnp.int32, (QB, cols), 1)
        return (keys <= rows) & (keys >= begin)

    return mask


def masked_scores(q2, keys, index, start, width, len0):
    s = nt(q2, keys)
    mask = score_mask(index, start, len0)
    causal_from = ((index * QB - start) // PAD) * PAD
    if index == 3:
        pieces = [(0, width, True)]
    elif index < 3:
        pieces = [(0, causal_from, False), (causal_from, width - causal_from, True)]
    elif causal_from <= 256:
        pieces = [(0, width, True)]
    else:
        pieces = [(0, 256, True), (256, causal_from - 256, False), (causal_from, width - causal_from, True)]
    halves = []
    for head in range(2):
        sh = s[head * QB : (head + 1) * QB]
        cols = []
        for col, n, masked in pieces:
            if n <= 0:
                continue
            part = sh[:, col : col + n]
            cols.append(jnp.where(mask(col, n), part, NEG) if masked else part)
        halves.append(cols[0] if len(cols) == 1 else jnp.concatenate(cols, axis=1))
    return halves


def attn_fwd_body(order, meta, q_ref, kv_ref, wo_ref, *rest):
    o_ref, lse_ref, near_ref, far_ref, o_acc = rest[-5:]
    step = pl.program_id(0)
    kvh = pl.program_id(1)
    index = order[step]
    scale = HD ** (-0.5)

    def block(i):
        start, width = SPANS[i]
        q2 = jnp.concatenate([q_ref[:, :PAD], q_ref[:, PAD:]], axis=0)
        keys = kv_ref[start : start + width, :PAD]
        values = kv_ref[start : start + width, PAD:]
        halves = masked_scores(q2, keys, i, start, width, meta[0])
        alive = i * QB + lax.broadcasted_iota(jnp.int32, (QB, 1), 0) < meta[1]
        for head in range(2):
            s = halves[head]
            top = jnp.max(s, axis=1, keepdims=True)
            e = jnp.exp2((s - top) * (scale * LOG2E))
            total = jnp.sum(e, axis=1, keepdims=True)
            p = (e * (1.0 / total)).astype(BF16)
            out = nn(p, values)
            o_acc[kvh * 2 + head] = jnp.where(alive, out, 0.0).astype(BF16)
            lse = top * (scale * LOG2E) + jnp.log2(total)
            lse_ref[:, head * 64 : (head + 1) * 64] = jnp.broadcast_to(lse, (QB, 64))

    for i in range(8):
        pl.when(index == i)(functools.partial(block, i))

    @pl.when(kvh == 1)
    def _():
        o = jnp.concatenate([o_acc[h] for h in range(4)], axis=1)
        o_ref[...] = o
        part = nt(o, wo_ref[...]).astype(BF16)

        @pl.when(step < 2)
        def _():
            near_ref[...] = part

        @pl.when(step >= 2)
        def _():
            far_ref[...] = part


def attn_fwd_call(order, meta, qkv, wop, earlier):
    total, _ = qkv.shape
    d = wop.shape[0]
    specs = [
        pl.BlockSpec((QB, 2 * PAD), lambda i, h, o, m: (o[i], 2 * h)),
        pl.BlockSpec((total, 2 * PAD), lambda i, h, o, m: (0, 2 * h + 1)),
        pl.BlockSpec(wop.shape, lambda i, h, o, m: (0, 0)),
    ]
    args = [order, meta, qkv, qkv, wop]
    alias = {}
    if earlier is not None:
        specs += [pl.BlockSpec(memory_space=pl.ANY)] * 2
        alias = {5: 0, 6: 1}
        args += list(earlier)
    return pl.pallas_call(
        attn_fwd_body,
        grid_spec=pltpu.PrefetchScalarGridSpec(
            num_scalar_prefetch=2,
            grid=(4, 2),
            in_specs=specs,
            out_specs=[
                pl.BlockSpec((QB, 4 * PAD), lambda i, h, o, m: (o[i], 0)),
                pl.BlockSpec((QB, PAD), lambda i, h, o, m: (o[i], h)),
                pl.BlockSpec((QB, d), lambda i, h, o, m: (jnp.minimum(i, 1), 0)),
                pl.BlockSpec((QB, d), lambda i, h, o, m: (jnp.maximum(i - 2, 0), 0)),
            ],
            scratch_shapes=[pltpu.VMEM((4, QB, PAD), BF16)],
        ),
        out_shape=[
            jax.ShapeDtypeStruct((total, 4 * PAD), BF16),
            jax.ShapeDtypeStruct((total, 2 * PAD), F32),
            jax.ShapeDtypeStruct((total // 4, d), BF16),
            jax.ShapeDtypeStruct((total // 4, d), BF16),
        ],
        input_output_aliases=alias,
        compiler_params=params(),
        cost_estimate=cost(9e9, 12e6, 5e6),
        name="attn_fwd",
    )(*args)


def attn_bwd_body(meta, q_ref, kv_ref, do_ref, lse_ref, cos, sin, cos_all, sin_all, out_ref, dk_acc, dv_acc):
    step = pl.program_id(0)
    scale = HD ** (-0.5)

    @pl.when(step == 0)
    def _():
        dk_acc[...] = jnp.zeros_like(dk_acc)
        dv_acc[...] = jnp.zeros_like(dv_acc)

    def block(i):
        start, width = SPANS[i]
        q2 = jnp.concatenate([q_ref[:, :PAD], q_ref[:, PAD:]], axis=0)
        do2 = jnp.concatenate([do_ref[:, :PAD], do_ref[:, PAD:]], axis=0)
        keys = kv_ref[start : start + width, :PAD]
        values = kv_ref[start : start + width, PAD:]
        halves = masked_scores(q2, keys, i, start, width, meta[0])
        dp2 = nt(do2, values)
        ps, dss = [], []
        for head in range(2):
            lse = lse_ref[:, head * 64 : head * 64 + 1]
            p = jnp.exp2(halves[head] * (scale * LOG2E) - lse)
            dp = dp2[head * QB : (head + 1) * QB]
            delta = jnp.sum(p * dp, axis=1, keepdims=True)
            dss.append((p * (dp - delta)).astype(BF16))
            ps.append(p.astype(BF16))
        pb = jnp.concatenate(ps, axis=0)
        ds = jnp.concatenate(dss, axis=0)
        dv_acc[start : start + width, :] += tn(pb, do2)
        dk_acc[start : start + width, :] += tn(ds, q2)
        dq = nn(ds, keys) * scale
        c, s = cos[...], sin[...]
        for head in range(2):
            part = dq[head * QB : (head + 1) * QB]
            part = part * c - pltpu.roll(part, 64, 1) * s
            out_ref[i * QB : (i + 1) * QB, head * PAD : (head + 1) * PAD] = part.astype(BF16)

    for i in range(8):
        pl.when(step == i)(functools.partial(block, i))

    @pl.when(step == 7)
    def _():
        dk = dk_acc[...] * scale
        dk = dk * cos_all[...] - pltpu.roll(dk, 64, 1) * sin_all[...]
        out_ref[:, 2 * PAD : 3 * PAD] = dk.astype(BF16)
        out_ref[:, 3 * PAD : 4 * PAD] = dv_acc[...].astype(BF16)


def attn_bwd_call(h, meta, qkv, dheads, lse, cos, sin):
    total, _ = qkv.shape
    return pl.pallas_call(
        attn_bwd_body,
        grid_spec=pltpu.PrefetchScalarGridSpec(
            num_scalar_prefetch=1,
            grid=(8,),
            in_specs=[
                pl.BlockSpec((QB, 2 * PAD), lambda i, m: (i, 2 * h)),
                pl.BlockSpec((total, 2 * PAD), lambda i, m: (0, 2 * h + 1)),
                pl.BlockSpec((QB, 2 * PAD), lambda i, m: (i, h)),
                pl.BlockSpec((QB, PAD), lambda i, m: (i, h)),
                pl.BlockSpec((QB, PAD), lambda i, m: (i, 0)),
                pl.BlockSpec((QB, PAD), lambda i, m: (i, 0)),
                pl.BlockSpec((total, PAD), lambda i, m: (0, 0)),
                pl.BlockSpec((total, PAD), lambda i, m: (0, 0)),
            ],
            out_specs=pl.BlockSpec((total, 4 * PAD), lambda i, m: (0, 0)),
            scratch_shapes=[pltpu.VMEM((total, PAD), F32), pltpu.VMEM((total, PAD), F32)],
        ),
        out_shape=jax.ShapeDtypeStruct((total, 4 * PAD), BF16),
        compiler_params=params(),
        cost_estimate=cost(15e9, 12e6, 5e6),
        name="attn_bwd",
    )(meta, qkv, qkv, dheads, lse, cos, sin, cos, sin)


def mlp_body(a0, a1, c0, c1, w_ref, hid_out, dg_out, du_out, mo_near, mo_far, da_near, da_far):
    first = pl.program_id(0) < pl.num_programs(0) // 2
    act = jnp.where(first, a0[...], a1[...])
    cot = jnp.where(first, c0[...], c1[...])
    ff = w_ref.shape[1] // 3
    wg, wu, wd = w_ref[:, :ff], w_ref[:, ff : 2 * ff], w_ref[:, 2 * ff :]
    gate = nn(act, wg)
    up = nn(act, wu)
    dh = nn(cot, wd)
    sig = 1.0 / (1.0 + jnp.exp(-gate))
    gs = gate * sig
    hid = (gs * up).astype(BF16)
    dg = (dh * up * sig * (1.0 + gate * (1.0 - sig))).astype(BF16)
    du = (dh * gs).astype(BF16)
    hid_out[...] = hid
    dg_out[...] = dg
    du_out[...] = du
    mo = nt(hid, wd).astype(BF16)
    da = (nt(dg, wg) + nt(du, wu)).astype(BF16)

    @pl.when(first)
    def _():
        mo_near[...] = mo
        da_near[...] = da

    @pl.when(jnp.logical_not(first))
    def _():
        mo_far[...] = mo
        da_far[...] = da


def mlp_call(a0, a1, c0, c1, w):
    rows, d = a0.shape
    ff = w.shape[1] // 3
    parts = 2
    bm = rows // parts
    lo = lambda i: (jnp.minimum(i, parts - 1), 0)
    hi = lambda i: (jnp.maximum(i - parts, 0), 0)
    return pl.pallas_call(
        mlp_body,
        grid=(2 * parts,),
        in_specs=[
            pl.BlockSpec((bm, d), lo),
            pl.BlockSpec((bm, d), hi),
            pl.BlockSpec((bm, d), lo),
            pl.BlockSpec((bm, d), hi),
            pl.BlockSpec(w.shape, lambda i: (0, 0), pipeline_mode=pl.Buffered(1)),
        ],
        out_specs=[pl.BlockSpec((bm, ff), lambda i: (i, 0))] * 3
        + [pl.BlockSpec((bm, d), lo), pl.BlockSpec((bm, d), hi)] * 2,
        out_shape=[jax.ShapeDtypeStruct((2 * rows, ff), BF16)] * 3
        + [jax.ShapeDtypeStruct((rows, d), BF16)] * 4,
        compiler_params=params(),
        cost_estimate=cost(12 * 2 * rows * d * ff, 2 * rows * (8 * d + 6 * ff) + w.size * 2, 2 * rows * ff),
        name="mlp_both",
    )(a0, a1, c0, c1, w)


def mlp_grad_body(count, where, a0, a1, a2, a3, *refs):
    mine, theirs = refs[-2:]
    step = pl.program_id(0)
    per = pl.num_programs(0) // count
    rows = a0.shape[0]

    def total(lo, hi):
        acc = tn(a0[...], lo[:rows])
        acc = acc + tn(a1[...], lo[rows:])
        acc = acc + tn(a2[...], hi[:rows])
        acc = acc + tn(a3[...], hi[rows:])
        pair_split(acc, where, mine, theirs)

    for k in range(count):
        pl.when(step // per == k)(functools.partial(total, refs[2 * k], refs[2 * k + 1]))


def mlp_grad_call(where, left, rights):
    rows, d = left[0].shape
    ff = rights[0][0].shape[1]
    per = 4
    bn = ff // per
    count = len(rights)
    whole = pl.BlockSpec((rows, d), lambda i, w: (0, 0), pipeline_mode=pl.Buffered(1))

    def part(k):
        return pl.BlockSpec((2 * rows, bn), lambda i, w: (0, jnp.clip(i - k * per, 0, per - 1)))

    return pl.pallas_call(
        functools.partial(mlp_grad_body, count),
        grid_spec=pltpu.PrefetchScalarGridSpec(
            num_scalar_prefetch=1,
            grid=(count * per,),
            in_specs=[whole] * 4 + [part(k) for k in range(count) for _ in range(2)],
            out_specs=[pl.BlockSpec((d // 2, bn), lambda i, w: (0, i))] * 2,
        ),
        out_shape=[jax.ShapeDtypeStruct((d // 2, count * ff), BF16)] * 2,
        compiler_params=params(),
        cost_estimate=cost(count * 8 * rows * d * ff, 8 * rows * d + count * (8 * rows * ff + 2 * d * ff)),
    )(where, *left, *[r for pair in rights for r in pair])


def heads_grad_body(order, meta, where, d0, d1, d2, d3, o_ref, wo_ref, un_ref, dh_out, g_mine, g_theirs, acc):
    step = pl.program_id(0)

    def piece(ref, first):
        dmid = ref[...]
        rows = dmid.shape[0]
        row = order[step] * rows + lax.broadcasted_iota(jnp.int32, (rows, 1), 0)
        dh = nn(dmid, wo_ref[...])
        dh_out[...] = jnp.where(row < meta[1], dh, 0.0).astype(BF16)
        g = tn(dmid, o_ref[...])
        if first:
            acc[...] = g
        else:
            acc[...] += g

    for k, ref in enumerate((d0, d1, d2, d3)):
        pl.when(step == k)(functools.partial(piece, ref, k == 0))

    @pl.when(step == 3)
    def _():
        pair_split(nt(acc[...].astype(BF16), un_ref[...]), where, g_mine, g_theirs)


def heads_grad_call(order, meta, where, pieces, o, wop, spread):
    rows, d = pieces[0].shape
    hw = o.shape[1]
    own = (d // 2, spread.shape[0])
    whole = lambda shape: pl.BlockSpec(shape, lambda i, o, m, w: (0, 0))
    block = pl.BlockSpec((rows, hw), lambda i, o, m, w: (o[i], 0))
    return pl.pallas_call(
        heads_grad_body,
        grid_spec=pltpu.PrefetchScalarGridSpec(
            num_scalar_prefetch=3,
            grid=(4,),
            in_specs=[whole((rows, d))] * 4 + [block, whole(wop.shape), whole(spread.shape)],
            out_specs=[block, whole(own), whole(own)],
            scratch_shapes=[pltpu.VMEM((d, hw), F32)],
        ),
        out_shape=[jax.ShapeDtypeStruct((4 * rows, hw), BF16)] + [jax.ShapeDtypeStruct(own, BF16)] * 2,
        compiler_params=params(),
        cost_estimate=cost(4 * 4 * rows * d * hw, 8 * rows * d + 16 * rows * hw + 4 * d * hw),
        name="heads_grad",
    )(order, meta, where, *pieces, o, wop, spread)


def act1_grad_body(order, g0_ref, g1_ref, w_ref, *outs):
    half = g0_ref.shape[1]
    y = (nt(g0_ref[...], w_ref[:, :half]) + nt(g1_ref[...], w_ref[:, half:])).astype(BF16)
    for k in range(4):
        def store(out):
            out[...] = y

        pl.when(pl.program_id(0) // 2 == k)(functools.partial(store, outs[k]))


def act1_grad_call(order, dqkv, wp):
    total, half = dqkv[0].shape
    d = wp.shape[0]
    rows = total // 8
    return pl.pallas_call(
        act1_grad_body,
        grid_spec=pltpu.PrefetchScalarGridSpec(
            num_scalar_prefetch=1,
            grid=(8,),
            in_specs=[
                pl.BlockSpec((rows, half), lambda i, o: (o[i], 0)),
                pl.BlockSpec((rows, half), lambda i, o: (o[i], 0)),
                pl.BlockSpec(wp.shape, lambda i, o: (0, 0)),
            ],
            out_specs=[
                pl.BlockSpec((rows, d), functools.partial(lambda k, i, o: (jnp.clip(i - 2 * k, 0, 1), 0), k))
                for k in range(4)
            ],
        ),
        out_shape=[jax.ShapeDtypeStruct((2 * rows, d), BF16)] * 4,
        compiler_params=params(),
        cost_estimate=cost(4 * total * half * d, 2 * total * (2 * half + d)),
        name="act1_grad",
    )(order, *dqkv, wp)


def qkv_grad_body(where, a_ref, g_ref, un_ref, mine, theirs, acc):
    step = pl.program_id(0)
    g = tn(a_ref[...], g_ref[...])

    @pl.when(step == 0)
    def _():
        acc[...] = g

    @pl.when(step > 0)
    def _():
        acc[...] += g

    @pl.when(step == pl.num_programs(0) - 1)
    def _():
        pair_split(nt(acc[...].astype(BF16), un_ref[...]), where, mine, theirs)


def qkv_grad_call(where, act, dqkv, spread):
    total, d = act.shape
    width = dqkv.shape[1]
    rows = total // 4
    own = (d // 2, spread.shape[0])
    whole = lambda shape: pl.BlockSpec(shape, lambda i, w: (0, 0))
    return pl.pallas_call(
        qkv_grad_body,
        grid_spec=pltpu.PrefetchScalarGridSpec(
            num_scalar_prefetch=1,
            grid=(4,),
            in_specs=[
                pl.BlockSpec((rows, d), lambda i, w: (i, 0)),
                pl.BlockSpec((rows, width), lambda i, w: (i, 0)),
                whole(spread.shape),
            ],
            out_specs=[whole(own)] * 2,
            scratch_shapes=[pltpu.VMEM((d, width), F32)],
        ),
        out_shape=[jax.ShapeDtypeStruct(own, BF16)] * 2,
        compiler_params=params(),
        cost_estimate=cost(2 * total * d * width, 2 * total * (d + width)),
        name="qkv_grad",
    )(where, act, dqkv, spread)


def on_device(
    block_in, cotangent, seq_lengths, seq_offsets, tok_counts, norm1_gain, norm2_gain,
    w_query, w_key, w_value, w_out, w_gate, w_up, w_down,
):
    rows, d = block_in.shape
    group_rows = rows * 4
    me = lax.axis_index("tensor")
    qc = w_query.shape[1]
    ff = w_gate.shape[1]

    near = jnp.stack([me, me ^ 1, me ^ 2, me ^ 3]).astype(jnp.int32)
    half_blocks = (near[:, None] * 2 + jnp.arange(2, dtype=jnp.int32)[None, :]).reshape(8)
    len0 = seq_lengths[0, 0]
    total = seq_lengths[0, 0] + seq_lengths[0, 1]
    meta = jnp.stack([len0, total]).astype(jnp.int32)
    mine = lax.axis_index("dp")
    pairs = lax.axis_size("dp") // 2
    where = jnp.stack([mine % 2, mine // 2]).astype(jnp.int32)
    piece = jnp.arange(2 * pairs, dtype=jnp.int32)
    piece_order = (2 * ((mine // 2 - piece // 2 + pairs) % pairs) + ((mine % 2) ^ (piece % 2))).astype(jnp.int32)

    x_peer = to_peer(block_in)
    x_partner = to_partner(block_in)
    gains = jnp.pad(jnp.stack([norm1_gain, norm2_gain], axis=1), ((0, 0), (0, PAD - 2)))
    w_first = jnp.concatenate([w_query, w_key, w_value, w_out.T, gains], axis=1)
    first_pieces = gather_pieces(w_first)
    w_second = jnp.concatenate([w_gate, w_up, w_down.T], axis=1)
    second_all = lax.all_gather(w_second, "dp", axis=0, tiled=True)
    x_diag = to_partner(x_peer)
    cot_peer = to_peer(cotangent)
    cot_partner = to_partner(cotangent)
    cot_diag = to_partner(cot_peer)

    kw = 2 * HD
    sources = [[2 * h * HD, (2 * h + 1) * HD, qc + h * HD, qc + kw + h * HD] for h in range(2)]
    spread_qkv = head_spread(sources[0] + sources[1], qc + 2 * kw)
    spread_o = head_spread([0, HD, 2 * HD, 3 * HD], qc)
    spread_h = head_spread([0, HD, 2 * HD, 3 * HD], 4 * HD)
    wp, wop, gain_rows = prep_call(piece_order, first_pieces, spread_qkv, spread_o)
    gain1 = gain_rows[:, 0, :].reshape(1, d)
    gain2 = gain_rows[:, 1, :].reshape(1, d)

    row_index = jnp.arange(group_rows, dtype=jnp.int32)
    position = jnp.where(
        row_index < len0, row_index, jnp.where(row_index < total, row_index - len0, 0)
    ).astype(F32)
    frequency = THETA ** (-jnp.arange(HALF, dtype=F32) * 2.0 / HD)
    angles = position[:, None] * frequency[None, :]
    cosines, sines = jnp.cos(angles), jnp.sin(angles)
    gap = jnp.zeros((group_rows, 64 - HALF), F32)
    cos = jnp.concatenate([cosines, gap, cosines, gap], axis=1)
    sin = jnp.concatenate([-sines, gap, sines, gap], axis=1)

    earlier = qkv_call(half_blocks[:4], meta, block_in, x_partner, gain1, wp, cos, sin, None)
    act1, qkv = qkv_call(half_blocks[4:], meta, x_peer, x_diag, gain1, wp, cos, sin, earlier)
    o_first, lse_first, at_peer, at_diag = attn_fwd_call(half_blocks[4:], meta, qkv, wop, None)
    o_all, lse, at_own, at_partner = attn_fwd_call(
        half_blocks[:4], meta, qkv, wop, (o_first, lse_first)
    )
    at_in = to_partner(at_diag)
    at_sum = (at_peer.astype(F32) + at_in.astype(F32)).astype(BF16)
    from_peer = to_peer(at_sum)
    from_partner = to_partner(at_partner)

    row_live = (me * rows + jnp.arange(rows, dtype=jnp.int32) < total)[:, None]
    xin = jnp.where(row_live, block_in.astype(F32), 0.0)
    mid = xin + (at_own.astype(F32) + from_partner.astype(F32) + from_peer.astype(F32))
    factor2 = lax.rsqrt(jnp.mean(mid * mid, axis=1, keepdims=True) + EPS)
    act2 = (mid * factor2 * gain2).astype(BF16)
    act2_peer = to_peer(act2)
    act2_partner = to_partner(act2)
    act2_diag = to_partner(act2_peer)

    hid_a, dg_a, du_a, mo_own, mo_partner, da_own, da_partner = mlp_call(
        act2, act2_partner, cotangent, cot_partner, second_all
    )
    hid_b, dg_b, du_b, mo_peer, mo_diag, da_peer, da_diag = mlp_call(
        act2_peer, act2_diag, cot_peer, cot_diag, second_all
    )
    da_in = to_partner(da_diag)
    da_sum = (da_peer.astype(F32) + da_in.astype(F32)).astype(BF16)
    da_from_peer = to_peer(da_sum)
    da_from_partner = to_partner(da_partner)
    dact2 = da_own.astype(F32) + da_from_partner.astype(F32) + da_from_peer.astype(F32)
    normed2 = mid * factor2
    dn2 = dact2 * gain2
    inner2 = jnp.mean(dn2 * normed2, axis=1, keepdims=True)
    dmid = cotangent.astype(F32) + factor2 * (dn2 - normed2 * inner2)
    dmid_low = dmid.astype(BF16)
    dmid_peer = to_peer(dmid_low)
    dmid_partner = to_partner(dmid_low)
    dmid_diag = to_partner(dmid_peer)

    cots = (cotangent, cot_partner, cot_peer, cot_diag)
    acts = (act2, act2_partner, act2_peer, act2_diag)
    gd_mine, gd_theirs = mlp_grad_call(where, cots, [(hid_a, hid_b)])
    gu_mine, gu_theirs = mlp_grad_call(where, acts, [(dg_a, dg_b), (du_a, du_b)])
    g_down = reduce_pieces(gd_mine, gd_theirs)
    g_up = reduce_pieces(gu_mine, gu_theirs)

    mo_in = to_partner(mo_diag)
    mo_sum = (mo_peer.astype(F32) + mo_in.astype(F32)).astype(BF16)
    mo_from_peer = to_peer(mo_sum)
    mo_from_partner = to_partner(mo_partner)
    dheads, go_mine, go_theirs = heads_grad_call(
        near, meta, where,
        (dmid_low, dmid_partner, dmid_peer, dmid_diag), o_all, wop, spread_o,
    )
    late_mid, _ = lax.optimization_barrier((mid, dheads))
    block_out = (
        late_mid + (mo_own.astype(F32) + mo_from_partner.astype(F32) + mo_from_peer.astype(F32))
    ).astype(BF16)
    dqkv = [attn_bwd_call(h, meta, qkv, dheads, lse, cos, sin) for h in range(2)]
    back_order = jnp.concatenate([half_blocks[4:], half_blocks[2:4], half_blocks[:2]])
    bk_peer, bk_diag, bk_partner, bk_own = act1_grad_call(back_order, dqkv, wp)
    bk_in = to_partner(bk_diag)
    bk_sum = (bk_peer.astype(F32) + bk_in.astype(F32)).astype(BF16)
    bk_from_peer = to_peer(bk_sum)
    bk_from_partner = to_partner(bk_partner)
    gq = [qkv_grad_call(where, act1, dqkv[h], spread_h) for h in range(2)]
    g_out = reduce_pieces(go_mine, go_theirs)
    g_heads = [reduce_pieces(*gq[h]) for h in range(2)]

    dact1 = bk_own.astype(F32) + bk_from_partner.astype(F32) + bk_from_peer.astype(F32)
    factor1 = lax.rsqrt(jnp.mean(xin * xin, axis=1, keepdims=True) + EPS)
    normed1 = xin * factor1
    dn1 = dact1 * gain1
    inner1 = jnp.mean(dn1 * normed1, axis=1, keepdims=True)
    grad_input = jnp.where(row_live, dmid + factor1 * (dn1 - normed1 * inner1), 0.0)

    g_q = jnp.concatenate([g[:, : 2 * HD] for g in g_heads], axis=1)
    g_k = jnp.concatenate([g[:, 2 * HD : 3 * HD] for g in g_heads], axis=1)
    g_v = jnp.concatenate([g[:, 3 * HD :] for g in g_heads], axis=1)
    dot1 = (
        jnp.sum(g_q * w_query.astype(F32), axis=1)
        + jnp.sum(g_k * w_key.astype(F32), axis=1)
        + jnp.sum(g_v * w_value.astype(F32), axis=1)
    )
    dot2 = jnp.sum(g_up[:, :ff] * w_gate.astype(F32) + g_up[:, ff:] * w_up.astype(F32), axis=1)
    dots = lax.psum(jnp.stack([dot1, dot2]), "tensor")
    return (
        block_out,
        grad_input,
        dots[0] / norm1_gain.astype(F32),
        dots[1] / norm2_gain.astype(F32),
        g_q,
        g_k,
        g_v,
        g_out.T,
        g_up[:, :ff],
        g_up[:, ff:],
        g_down.T,
    )


def solution(mesh):
    in_specs = (
        P(("dp", "tensor"), None),
        P(("dp", "tensor"), None),
        P("dp", None),
        P("dp", None),
        P("dp", "tensor"),
        P("dp"),
        P("dp"),
        P("dp", "tensor"),
        P("dp", "tensor"),
        P("dp", "tensor"),
        P("tensor", "dp"),
        P("dp", "tensor"),
        P("dp", "tensor"),
        P("tensor", "dp"),
    )
    out_specs = (
        P(("dp", "tensor"), None),
        P(("dp", "tensor"), None),
        P("dp"),
        P("dp"),
        P("dp", "tensor"),
        P("dp", "tensor"),
        P("dp", "tensor"),
        P("tensor", "dp"),
        P("dp", "tensor"),
        P("dp", "tensor"),
        P("tensor", "dp"),
    )
    return jax.shard_map(on_device, mesh=mesh, in_specs=in_specs, out_specs=out_specs, check_vma=False)
```
